32 devices in a mesh: pipe: 8 (over z, core), expert: 4 (over y, x).
Axes of the slice: x: 2, y: 2, z: 4, core: 2. Of those that a mesh axis runs over, the one named last changes fastest.
Arguments:
- acts: bfloat16 [8, 512, 3584], P('pipe', 'expert'), may hold values from -6 to 6
- routing: int32 [8, 512, 8], P('pipe', 'expert'), may hold values from 0 to 255, as said below
- combine_w: float32 [8, 512, 8], P('pipe', 'expert'), may hold values from 0.25 to 2.5
- w_gate_up: bfloat16 [8, 3584, 4096], P('pipe', None, 'expert'), may hold values from -0.09375 to 0.09375
- w_down: bfloat16 [8, 2048, 3584], P('pipe', 'expert'), may hold values from -0.125 to 0.125
Outputs:
- next_acts: bfloat16 [8, 512, 3584], P('pipe', 'expert')
The draws below stay inside these ranges and needn't reach their ends.
Inputs may be any that keep to these rules, and one draw needn't show every extreme that they name: `routing`: each row names 8 different experts. Within one section every aligned block of 128 rows (the rows of one device) holds the same number of rows naming expert 0, at least 1 and at most 8; in one section of every draw, drawn from the seed, exactly 8.
All inputs are finite; a program needn't handle non-finite values.
Results may differ from the reference program's by a relative error of at most 0.0055.
Values may be sent and summed in bfloat16 or wider, within the bound.
A program may use at most 64 MiB of HBM per device.

```python
import jax
import jax.numpy as jnp
from jax import lax

D = 3584
FF = 2048
ROUTED = 256
TOPK = 8
TOK_DEV = 128
CAP = 8
SECT = 8
TOKENS = 512
HID_DEV = 512
N_EXPERT = 4


def draw_routing(key, part):
    per_section = TOKENS // TOK_DEV
    blocks = per_section * SECT
    key_list = jax.random.split(key, 6)
    columns = jnp.arange(ROUTED)
    scores = jax.random.randint(key_list[1], (blocks, TOK_DEV, ROUTED), 0, 1 << 20) * ROUTED + columns
    scores = jnp.where(columns < 1, -1, scores)
    fillers = lax.top_k(scores, TOPK)[1].astype(jnp.int32)
    first_keys = jax.random.randint(key_list[2], (blocks, TOK_DEV), 0, 1 << 20) * TOK_DEV + jnp.arange(TOK_DEV)
    first_rank = jnp.argsort(jnp.argsort(first_keys, axis=1), axis=1)
    counts = jax.random.randint(key_list[3], (SECT, 1), 1, CAP + 1)
    full_section = jax.random.randint(key_list[0], (), 0, SECT)
    counts = jnp.where(jnp.arange(SECT)[:, None] == full_section, CAP, counts)
    block_counts = jnp.repeat(counts, per_section, axis=0)
    in_hot = first_rank < block_counts
    column_zero = jnp.where(in_hot, 0, fillers[..., 0])
    listed = jnp.concatenate([column_zero[..., None], fillers[..., 1:]], axis=-1)
    shuffle_keys = jax.random.randint(key_list[5], (blocks, TOK_DEV, TOPK), 0, 1 << 20) * TOPK + jnp.arange(TOPK)
    shuffle_order = jnp.argsort(shuffle_keys, axis=-1)
    listed = jnp.take_along_axis(listed, shuffle_order, axis=-1)
    return listed.reshape(SECT, TOKENS, TOPK).astype(jnp.int32)


def block_levels(own_key, extent, cuts, smallest, top_value):
    loudness, own = 1.0, jax.random.fold_in(own_key, 6)
    for dim, shards_of in cuts:
        steps = jnp.exp(jax.random.uniform(jax.random.fold_in(own, dim), (shards_of,), jnp.float32, smallest / len(cuts), top_value / len(cuts)))
        loudness = loudness * jnp.repeat(steps, extent[dim] // shards_of).reshape([-1 if axis == dim else 1 for axis in range(len(extent))])
    return loudness


def normal_values(key, dims, spread, most, cuts=(), held_as=jnp.bfloat16):
    level = block_levels(key, dims, cuts, -0.22, 0.18) if cuts else 1.0
    entries = jax.random.normal(key, dims, jnp.float32) * spread * level
    return jnp.minimum(jnp.maximum(entries, -most), most).astype(held_as)


def setup_inputs(seed: int = 0) -> dict:
    streams_of = jax.random.split(jax.random.key(seed), 6)
    return {
        "acts": normal_values(streams_of[0], (SECT, TOKENS, D), 1.0, 6.0, ((0, 8), (1, 4))),
        "routing": draw_routing(jax.random.fold_in(streams_of[5], 71), 0),
        "combine_w": jnp.clip(0.25 + 2.25 * jax.random.uniform(streams_of[2], (SECT, TOKENS, TOPK), jnp.float32) ** block_levels(streams_of[2], (SECT, TOKENS, TOPK), ((0, 8), (1, 4)), -0.2, 0.2), 0.25, 2.5),
        "w_gate_up": normal_values(streams_of[3], (SECT, D, 2 * FF), D ** -0.5, 0.09375, ((0, 8), (2, 4))),
        "w_down": normal_values(streams_of[4], (SECT, FF, D), FF ** -0.5, 0.125, ((0, 8), (1, 4))),
    }


def section_layer(tokens_in, route_ids, mix_weights, w_gate_up, w_down):
    row_count = N_EXPERT * CAP
    names_zero = route_ids == 0
    chosen = jnp.any(names_zero, axis=1)
    coefficient = jnp.sum(jnp.where(names_zero, mix_weights, 0.0), axis=1)
    picked = jnp.nonzero(chosen, size=row_count, fill_value=0)[0].astype(jnp.int32)
    valid_slot = jnp.arange(row_count, dtype=jnp.int32) < jnp.sum(chosen.astype(jnp.int32))
    rows_in = tokens_in[picked]
    paired = w_gate_up.reshape(D, N_EXPERT, 2, HID_DEV)
    gate_cols = paired[:, :, 0, :].reshape(D, FF)
    up_cols = paired[:, :, 1, :].reshape(D, FF)
    gate_part = jnp.dot(rows_in, gate_cols, preferred_element_type=jnp.float32)
    up_part = jnp.dot(rows_in, up_cols, preferred_element_type=jnp.float32)
    hidden = (jax.nn.silu(gate_part) * up_part).astype(jnp.bfloat16)
    blocks = hidden.astype(jnp.float32).reshape(row_count, N_EXPERT, HID_DEV)
    down_rows = w_down.astype(jnp.float32).reshape(N_EXPERT, HID_DEV, D)
    partial_value = jnp.einsum('ngh,ghd->ngd', blocks, down_rows).astype(jnp.bfloat16)
    merged = jnp.sum(partial_value.astype(jnp.float32), axis=1)
    scale_rows = jnp.where(valid_slot, coefficient[picked], 0.0)
    total_rows = jnp.zeros(tokens_in.shape, jnp.float32).at[picked].add(scale_rows[:, None] * merged)
    return (tokens_in.astype(jnp.float32) + total_rows).astype(jnp.bfloat16)


def reference(acts, routing, combine_w, w_gate_up, w_down):
    def one_section(section_items):
        return section_layer(*section_items)

    layers = lax.map(one_section, (acts, routing, combine_w, w_gate_up, w_down))
    return jnp.roll(layers, 1, axis=0)
```

```python
import functools

import jax
import jax.numpy as jnp
from jax import lax
from jax.experimental import pallas as pl
from jax.experimental.pallas import tpu as pltpu
from jax.sharding import PartitionSpec as P

CAP = 8
MESH = pl.DeviceIdType.MESH


def pieces_of(width):
    for count in (4, 2):
        if width % (128 * count) == 0:
            return count
    return 1


def kernel(
    stages,
    peers,
    pieces,
    out_pieces,
    acts,
    routing,
    combine_w,
    w_gate_up,
    w_down,
    landed,
    rows_out,
    select_out,
    acts_v,
    route_v,
    mix_v,
    gate_up_v,
    down_v,
    gathered,
    part_send,
    part_recv,
    table_send,
    table_recv,
    load_sem,
    gate_up_sem,
    down_sem,
    stream_sem,
    table_sem,
    gather_send_sem,
    gather_recv_sem,
    part_send_sem,
    part_recv_sem,
    ready_sem,
):
    stage = lax.axis_index("pipe")
    me = lax.axis_index("expert")
    after = lax.rem(stage + 1, stages)
    before = lax.rem(stage + stages - 1, stages)
    width = acts.shape[2]
    tokens = acts.shape[1]
    hid = w_down.shape[1]
    step = width // pieces

    load_route = pltpu.make_async_copy(routing.at[0], route_v, load_sem.at[0])
    load_mix = pltpu.make_async_copy(combine_w.at[0], mix_v, load_sem.at[1])
    load_acts = pltpu.make_async_copy(acts.at[0], acts_v, load_sem.at[2])
    load_route.start()
    load_mix.start()
    load_acts.start()
    gate_up_loads = []
    for p in range(pieces):
        rows = pl.ds(p * step, step)
        load = pltpu.make_async_copy(
            w_gate_up.at[0, rows, :], gate_up_v.at[rows, :], gate_up_sem.at[p]
        )
        load.start()
        gate_up_loads.append(load)
    load_down = pltpu.make_async_copy(w_down.at[0], down_v, down_sem)
    load_down.start()

    barrier = pltpu.get_barrier_semaphore()
    for k in range(1, peers):
        pl.semaphore_signal(
            barrier, inc=1, device_id=(stage, lax.rem(me + k, peers)), device_id_type=MESH
        )
    pl.semaphore_signal(barrier, inc=1, device_id=(before, me), device_id_type=MESH)
    pl.semaphore_signal(barrier, inc=1, device_id=(after, me), device_id_type=MESH)

    load_route.wait()
    load_mix.wait()
    named = route_v[...] == 0
    named_f = named.astype(jnp.float32)
    mix = jnp.where(named, mix_v[...], 0.0)
    chosen = lax.dot_general(
        jnp.ones((CAP, named_f.shape[1]), jnp.float32),
        named_f,
        (((1,), (1,)), ((), ())),
        preferred_element_type=jnp.float32,
    )
    earlier = (
        lax.broadcasted_iota(jnp.int32, (tokens, tokens), 0)
        <= lax.broadcasted_iota(jnp.int32, (tokens, tokens), 1)
    ).astype(jnp.float32)
    count = jnp.dot(chosen, earlier, preferred_element_type=jnp.float32)
    slot = lax.broadcasted_iota(jnp.int32, (CAP, tokens), 0).astype(jnp.float32) + 1.0
    select = jnp.where((count == slot) & (chosen > 0.5), 1.0, 0.0)
    slot_mix = jnp.dot(
        select, mix, preferred_element_type=jnp.float32, precision=lax.Precision.HIGHEST
    )
    slot_coeff = jnp.sum(slot_mix, axis=1, keepdims=True)
    table_send[...] = select * slot_coeff
    select_b = select.astype(jnp.bfloat16)

    load_acts.wait()
    for p in range(pieces):
        cols = pl.ds(p * step, step)
        gathered[me, :, cols] = jnp.dot(
            select_b, acts_v[:, cols], preferred_element_type=jnp.float32
        ).astype(jnp.bfloat16)

    pl.semaphore_wait(barrier, peers + 1)

    gathers = []
    for p in range(pieces):
        cols = pl.ds(p * step, step)
        for k in range(1, peers):
            copy = pltpu.make_async_remote_copy(
                src_ref=gathered.at[me, :, cols],
                dst_ref=gathered.at[me, :, cols],
                send_sem=gather_send_sem.at[p, k],
                recv_sem=gather_recv_sem.at[p, me],
                device_id=(stage, lax.rem(me + k, peers)),
                device_id_type=MESH,
            )
            copy.start()
            gathers.append(copy)
    stream = pltpu.make_async_remote_copy(
        src_ref=acts,
        dst_ref=landed,
        send_sem=stream_sem.at[0],
        recv_sem=stream_sem.at[1],
        device_id=(after, me),
        device_id_type=MESH,
    )
    stream.start()
    table = pltpu.make_async_remote_copy(
        src_ref=table_send,
        dst_ref=table_recv,
        send_sem=table_sem.at[0],
        recv_sem=table_sem.at[1],
        device_id=(after, me),
        device_id_type=MESH,
    )
    table.start()
    for k in range(1, peers):
        pl.semaphore_signal(
            ready_sem, inc=1, device_id=(stage, lax.rem(me + k, peers)), device_id_type=MESH
        )

    total = None
    for p in range(pieces):
        cols = pl.ds(p * step, step)
        gate_up_loads[p].wait()
        for k in range(1, peers):
            source = lax.rem(me + k, peers)
            pltpu.make_async_remote_copy(
                src_ref=gathered.at[source, :, cols],
                dst_ref=gathered.at[source, :, cols],
                send_sem=gather_send_sem.at[p, k],
                recv_sem=gather_recv_sem.at[p, source],
                device_id=(stage, source),
                device_id_type=MESH,
            ).wait_recv()
        rows = (
            gathered[:, :, cols]
            .astype(jnp.float32)
            .reshape(peers * CAP, step)
            .astype(jnp.bfloat16)
        )
        term = jnp.dot(
            rows, gate_up_v[pl.ds(p * step, step), :], preferred_element_type=jnp.float32
        )
        total = term if total is None else total + term
    gate = total[:, :hid]
    up = total[:, hid:]
    hidden = (gate / (1.0 + jnp.exp(-gate)) * up).astype(jnp.bfloat16)

    load_down.wait()
    if peers > 1:
        pl.semaphore_wait(ready_sem, peers - 1)
    out_step = width // out_pieces
    for p in range(out_pieces):
        cols = pl.ds(p * out_step, out_step)
        part = jnp.dot(hidden, down_v[:, cols], preferred_element_type=jnp.float32)
        part_send[:, :, cols] = part.reshape(peers, CAP, out_step).astype(jnp.bfloat16)
        for k in range(peers):
            owner = lax.rem(me + k, peers)
            pltpu.make_async_remote_copy(
                src_ref=part_send.at[owner, :, cols],
                dst_ref=part_recv.at[me, :, cols],
                send_sem=part_send_sem.at[k],
                recv_sem=part_recv_sem.at[me],
                device_id=(after, owner),
                device_id_type=MESH,
            ).start()

    table.wait()
    coeff_in = jnp.sum(table_recv[...], axis=1, keepdims=True)
    select_out[...] = jnp.where(table_recv[...] != 0.0, 1.0, 0.0).astype(jnp.bfloat16)
    for copy in gathers:
        copy.wait_send()
    stream.wait()
    for k in range(peers):
        source = lax.rem(me + k, peers)
        pltpu.make_async_remote_copy(
            src_ref=part_send.at[source],
            dst_ref=part_recv.at[source],
            send_sem=part_send_sem.at[k],
            recv_sem=part_recv_sem.at[source],
            device_id=(after, source),
            device_id_type=MESH,
        ).wait()
    merged = jnp.sum(part_recv[...].astype(jnp.float32), axis=0)
    rows_out[...] = (merged * coeff_in).astype(jnp.bfloat16)


def per_device(stages, peers, acts, routing, combine_w, w_gate_up, w_down):
    _, tokens, width = acts.shape
    hid = w_down.shape[1]
    pieces = pieces_of(width)
    out_pieces = pieces
    anywhere = pl.BlockSpec(memory_space=pl.ANY)
    in_vmem = pl.BlockSpec(memory_space=pltpu.VMEM)
    dma = pltpu.SemaphoreType.DMA
    landed, rows, select = pl.pallas_call(
        functools.partial(kernel, stages, peers, pieces, out_pieces),
        out_shape=(
            jax.ShapeDtypeStruct(acts.shape, acts.dtype),
            jax.ShapeDtypeStruct((CAP, width), jnp.bfloat16),
            jax.ShapeDtypeStruct((CAP, tokens), jnp.bfloat16),
        ),
        in_specs=[anywhere] * 5,
        out_specs=(anywhere, in_vmem, in_vmem),
        scratch_shapes=[
            pltpu.VMEM((tokens, width), acts.dtype),
            pltpu.VMEM(routing.shape[1:], routing.dtype),
            pltpu.VMEM(combine_w.shape[1:], combine_w.dtype),
            pltpu.VMEM(w_gate_up.shape[1:], w_gate_up.dtype),
            pltpu.VMEM(w_down.shape[1:], w_down.dtype),
            pltpu.VMEM((peers, CAP, width), jnp.bfloat16),
            pltpu.VMEM((peers, CAP, width), jnp.bfloat16),
            pltpu.VMEM((peers, CAP, width), jnp.bfloat16),
            pltpu.VMEM((CAP, tokens), jnp.float32),
            pltpu.VMEM((CAP, tokens), jnp.float32),
            dma((3,)),
            dma((pieces,)),
            dma,
            dma((2,)),
            dma((2,)),
            dma((pieces, peers)),
            dma((pieces, peers)),
            dma((peers,)),
            dma((peers,)),
            pltpu.SemaphoreType.REGULAR,
        ],
        compiler_params=pltpu.CompilerParams(collective_id=0, has_side_effects=True),
        name="relay_tick",
    )(acts, routing, combine_w, w_gate_up, w_down)
    layer = lax.dot_general(
        select, rows, (((0,), (0,)), ((), ())), preferred_element_type=jnp.float32
    )
    return (landed[0].astype(jnp.float32) + layer).astype(acts.dtype)[None]


def solution(mesh):
    return jax.shard_map(
        functools.partial(per_device, mesh.shape["pipe"], mesh.shape["expert"]),
        mesh=mesh,
        in_specs=(
            P("pipe", "expert", None),
            P("pipe", "expert", None),
            P("pipe", "expert", None),
            P("pipe", None, "expert"),
            P("pipe", "expert", None),
        ),
        out_specs=P("pipe", "expert", None),
        check_vma=False,
    )
```

```python
import functools

import jax
import jax.numpy as jnp
from jax import lax
from jax.experimental import pallas as pl
from jax.experimental.pallas import tpu as pltpu
from jax.sharding import PartitionSpec as P

CAP = 8
MESH = pl.DeviceIdType.MESH


def pieces_of(width):
    for count in (4, 2):
        if width % (128 * count) == 0:
            return count
    return 1


def kernel(
    stages,
    peers,
    pieces,
    out_pieces,
    acts,
    routing,
    combine_w,
    w_gate_up,
    w_down,
    out,
    landed,
    acts_v,
    route_v,
    mix_v,
    gate_up_v,
    down_v,
    gathered,
    part_send,
    part_recv,
    table_send,
    table_recv,
    load_sem,
    gate_up_sem,
    down_sem,
    stream_sem,
    table_sem,
    gather_send_sem,
    gather_recv_sem,
    part_send_sem,
    part_recv_sem,
    ready_sem,
):
    stage = lax.axis_index("pipe")
    me = lax.axis_index("expert")
    after = lax.rem(stage + 1, stages)
    before = lax.rem(stage + stages - 1, stages)
    width = acts.shape[2]
    tokens = acts.shape[1]
    hid = w_down.shape[1]
    step = width // pieces

    barrier = pltpu.get_barrier_semaphore()
    for k in range(1, peers):
        pl.semaphore_signal(
            barrier, inc=1, device_id=(stage, lax.rem(me + k, peers)), device_id_type=MESH
        )
    pl.semaphore_signal(barrier, inc=1, device_id=(before, me), device_id_type=MESH)
    pl.semaphore_signal(barrier, inc=1, device_id=(after, me), device_id_type=MESH)

    load_route = pltpu.make_async_copy(routing.at[0], route_v, load_sem.at[0])
    load_mix = pltpu.make_async_copy(combine_w.at[0], mix_v, load_sem.at[1])
    load_acts = pltpu.make_async_copy(acts.at[0], acts_v, load_sem.at[2])
    load_route.start()
    load_mix.start()
    load_acts.start()
    gate_up_loads = []
    for p in range(pieces):
        rows = pl.ds(p * step, step)
        load = pltpu.make_async_copy(
            w_gate_up.at[0, rows, :], gate_up_v.at[rows, :], gate_up_sem.at[p]
        )
        load.start()
        gate_up_loads.append(load)
    load_down = pltpu.make_async_copy(w_down.at[0], down_v, down_sem)
    load_down.start()

    load_route.wait()
    load_mix.wait()
    named = route_v[...] == 0
    chosen = jnp.max(jnp.where(named, 1.0, 0.0), axis=0, keepdims=True)
    coefficient = jnp.sum(jnp.where(named, mix_v[...], 0.0), axis=0, keepdims=True)
    earlier = (
        lax.broadcasted_iota(jnp.int32, (tokens, tokens), 0)
        <= lax.broadcasted_iota(jnp.int32, (tokens, tokens), 1)
    ).astype(jnp.float32)
    count = jnp.dot(
        jnp.broadcast_to(chosen, (CAP, tokens)), earlier, preferred_element_type=jnp.float32
    )
    slot = lax.broadcasted_iota(jnp.int32, (CAP, tokens), 0).astype(jnp.float32) + 1.0
    select = jnp.where((count == slot) & (chosen > 0.5), 1.0, 0.0)
    table_send[...] = select * coefficient
    select_b = select.astype(jnp.bfloat16)

    pl.semaphore_wait(barrier, peers + 1)
    stream = pltpu.make_async_remote_copy(
        src_ref=acts,
        dst_ref=landed,
        send_sem=stream_sem.at[0],
        recv_sem=stream_sem.at[1],
        device_id=(after, me),
        device_id_type=MESH,
    )
    stream.start()

    load_acts.wait()
    gathers = []
    for p in range(pieces):
        cols = pl.ds(p * step, step)
        gathered[me, :, cols] = jnp.dot(
            select_b, acts_v[:, cols], preferred_element_type=jnp.float32
        ).astype(jnp.bfloat16)
        for k in range(1, peers):
            copy = pltpu.make_async_remote_copy(
                src_ref=gathered.at[me, :, cols],
                dst_ref=gathered.at[me, :, cols],
                send_sem=gather_send_sem.at[p, k],
                recv_sem=gather_recv_sem.at[p, me],
                device_id=(stage, lax.rem(me + k, peers)),
                device_id_type=MESH,
            )
            copy.start()
            gathers.append(copy)
    table = pltpu.make_async_remote_copy(
        src_ref=table_send,
        dst_ref=table_recv,
        send_sem=table_sem.at[0],
        recv_sem=table_sem.at[1],
        device_id=(after, me),
        device_id_type=MESH,
    )
    table.start()
    for k in range(1, peers):
        pl.semaphore_signal(
            ready_sem, inc=1, device_id=(stage, lax.rem(me + k, peers)), device_id_type=MESH
        )

    total = None
    for p in range(pieces):
        cols = pl.ds(p * step, step)
        gate_up_loads[p].wait()
        for k in range(1, peers):
            source = lax.rem(me + k, peers)
            pltpu.make_async_remote_copy(
                src_ref=gathered.at[source, :, cols],
                dst_ref=gathered.at[source, :, cols],
                send_sem=gather_send_sem.at[p, k],
                recv_sem=gather_recv_sem.at[p, source],
                device_id=(stage, source),
                device_id_type=MESH,
            ).wait_recv()
        rows = (
            gathered[:, :, cols]
            .astype(jnp.float32)
            .reshape(peers * CAP, step)
            .astype(jnp.bfloat16)
        )
        term = jnp.dot(
            rows, gate_up_v[pl.ds(p * step, step), :], preferred_element_type=jnp.float32
        )
        total = term if total is None else total + term
    gate = total[:, :hid]
    up = total[:, hid:]
    hidden = (gate / (1.0 + jnp.exp(-gate)) * up).astype(jnp.bfloat16)

    load_down.wait()
    if peers > 1:
        pl.semaphore_wait(ready_sem, peers - 1)
    out_step = width // out_pieces
    for p in range(out_pieces):
        cols = pl.ds(p * out_step, out_step)
        part = jnp.dot(hidden, down_v[:, cols], preferred_element_type=jnp.float32)
        part_send[:, :, cols] = part.reshape(peers, CAP, out_step).astype(jnp.bfloat16)
        for k in range(peers):
            owner = lax.rem(me + k, peers)
            pltpu.make_async_remote_copy(
                src_ref=part_send.at[owner, :, cols],
                dst_ref=part_recv.at[me, :, cols],
                send_sem=part_send_sem.at[k],
                recv_sem=part_recv_sem.at[me],
                device_id=(after, owner),
                device_id_type=MESH,
            ).start()

    table.wait()
    coeff_in = jnp.sum(table_recv[...], axis=1, keepdims=True)
    spread = jnp.where(table_recv[...] != 0.0, 1.0, 0.0).astype(jnp.bfloat16)
    for copy in gathers:
        copy.wait_send()
    stream.wait()
    for k in range(peers):
        source = lax.rem(me + k, peers)
        pltpu.make_async_remote_copy(
            src_ref=part_send.at[source],
            dst_ref=part_recv.at[source],
            send_sem=part_send_sem.at[k],
            recv_sem=part_recv_sem.at[source],
            device_id=(after, source),
            device_id_type=MESH,
        ).wait()
    for p in range(out_pieces):
        cols = pl.ds(p * out_step, out_step)
        merged = jnp.sum(part_recv[:, :, cols].astype(jnp.float32), axis=0)
        rows = (merged * coeff_in).astype(jnp.bfloat16)
        layer = lax.dot_general(
            spread, rows, (((0,), (0,)), ((), ())), preferred_element_type=jnp.float32
        )
        out[0, :, cols] = (landed[0, :, cols].astype(jnp.float32) + layer).astype(out.dtype)


def per_device(stages, peers, acts, routing, combine_w, w_gate_up, w_down):
    _, tokens, width = acts.shape
    routing = jnp.swapaxes(routing, 1, 2)
    combine_w = jnp.swapaxes(combine_w, 1, 2)
    pieces = pieces_of(width)
    out_pieces = pieces
    anywhere = pl.BlockSpec(memory_space=pl.ANY)
    in_vmem = pl.BlockSpec(memory_space=pltpu.VMEM)
    dma = pltpu.SemaphoreType.DMA
    return pl.pallas_call(
        functools.partial(kernel, stages, peers, pieces, out_pieces),
        out_shape=pltpu.VMEM(acts.shape, acts.dtype),
        in_specs=[anywhere] * 5,
        out_specs=in_vmem,
        scratch_shapes=[
            pltpu.VMEM(acts.shape, acts.dtype),
            pltpu.VMEM((tokens, width), acts.dtype),
            pltpu.VMEM(routing.shape[1:], routing.dtype),
            pltpu.VMEM(combine_w.shape[1:], combine_w.dtype),
            pltpu.VMEM(w_gate_up.shape[1:], w_gate_up.dtype),
            pltpu.VMEM(w_down.shape[1:], w_down.dtype),
            pltpu.VMEM((peers, CAP, width), jnp.bfloat16),
            pltpu.VMEM((peers, CAP, width), jnp.bfloat16),
            pltpu.VMEM((peers, CAP, width), jnp.bfloat16),
            pltpu.VMEM((CAP, tokens), jnp.float32),
            pltpu.VMEM((CAP, tokens), jnp.float32),
            dma((3,)),
            dma((pieces,)),
            dma,
            dma((2,)),
            dma((2,)),
            dma((pieces, peers)),
            dma((pieces, peers)),
            dma((peers,)),
            dma((peers,)),
            pltpu.SemaphoreType.REGULAR,
        ],
        compiler_params=pltpu.CompilerParams(collective_id=0, has_side_effects=True),
        name="relay_tick",
    )(acts, routing, combine_w, w_gate_up, w_down)


def solution(mesh):
    return jax.shard_map(
        functools.partial(per_device, mesh.shape["pipe"], mesh.shape["expert"]),
        mesh=mesh,
        in_specs=(
            P("pipe", "expert", None),
            P("pipe", "expert", None),
            P("pipe", "expert", None),
            P("pipe", None, "expert"),
            P("pipe", "expert", None),
        ),
        out_specs=P("pipe", "expert", None),
        check_vma=False,
    )
```

```python
import functools

import jax
import jax.numpy as jnp
from jax import lax
from jax.experimental import pallas as pl
from jax.experimental.pallas import tpu as pltpu
from jax.sharding import PartitionSpec as P

CAP = 8
MESH = pl.DeviceIdType.MESH


def pieces_of(width):
    for count in (2,):
        if width % (128 * count) == 0:
            return count
    return 1


def kernel(
    stages,
    peers,
    pieces,
    row_pieces,
    acts,
    routing,
    combine_w,
    w_gate_up,
    w_down,
    out,
    landed,
    acts_v,
    route_v,
    mix_v,
    gate_up_v,
    down_v,
    gathered,
    part_send,
    part_recv,
    rows_send,
    rows_recv,
    table_send,
    table_recv,
    load_sem,
    gate_up_sem,
    down_sem,
    stream_sem,
    table_sem,
    gather_send_sem,
    gather_recv_sem,
    part_send_sem,
    part_recv_sem,
    rows_sem,
):
    stage = lax.axis_index("pipe")
    me = lax.axis_index("expert")
    after = lax.rem(stage + 1, stages)
    before = lax.rem(stage + stages - 1, stages)
    width = acts.shape[2]
    tokens = acts.shape[1]
    hid = w_down.shape[1]
    step = width // pieces
    row_step = tokens // row_pieces

    barrier = pltpu.get_barrier_semaphore()
    for k in range(1, peers):
        pl.semaphore_signal(
            barrier, inc=1, device_id=(stage, lax.rem(me + k, peers)), device_id_type=MESH
        )
    pl.semaphore_signal(barrier, inc=1, device_id=(before, me), device_id_type=MESH)
    pl.semaphore_signal(barrier, inc=1, device_id=(after, me), device_id_type=MESH)

    load_route = pltpu.make_async_copy(routing.at[0], route_v, load_sem.at[0])
    load_mix = pltpu.make_async_copy(combine_w.at[0], mix_v, load_sem.at[1])
    load_acts = pltpu.make_async_copy(acts.at[0], acts_v, load_sem.at[2])
    load_route.start()
    load_mix.start()
    load_acts.start()
    gate_up_loads = []
    for p in range(pieces):
        rows = pl.ds(p * step, step)
        load = pltpu.make_async_copy(
            w_gate_up.at[0, rows, :], gate_up_v.at[rows, :], gate_up_sem.at[p]
        )
        load.start()
        gate_up_loads.append(load)
    load_down = pltpu.make_async_copy(w_down.at[0], down_v, down_sem)
    load_down.start()

    pl.semaphore_wait(barrier, peers + 1)
    streams = []
    for p in range(row_pieces):
        span = pl.ds(p * row_step, row_step)
        stream = pltpu.make_async_remote_copy(
            src_ref=acts.at[:, span, :],
            dst_ref=landed.at[:, span, :],
            send_sem=stream_sem.at[0, p],
            recv_sem=stream_sem.at[1, p],
            device_id=(after, me),
            device_id_type=MESH,
        )
        stream.start()
        streams.append(stream)

    load_route.wait()
    load_mix.wait()
    named = route_v[...] == 0
    chosen = jnp.max(jnp.where(named, 1.0, 0.0), axis=0, keepdims=True)
    coefficient = jnp.sum(jnp.where(named, mix_v[...], 0.0), axis=0, keepdims=True)
    earlier = (
        lax.broadcasted_iota(jnp.int32, (tokens, tokens), 0)
        <= lax.broadcasted_iota(jnp.int32, (tokens, tokens), 1)
    ).astype(jnp.float32)
    count = jnp.dot(
        jnp.broadcast_to(chosen, (CAP, tokens)), earlier, preferred_element_type=jnp.float32
    )
    slot = lax.broadcasted_iota(jnp.int32, (CAP, tokens), 0).astype(jnp.float32) + 1.0
    select = jnp.where((count == slot) & (chosen > 0.5), 1.0, 0.0)
    slot_coeff = jnp.sum(select * coefficient, axis=1, keepdims=True)
    select_b = select.astype(jnp.bfloat16)
    table_send[...] = select_b

    load_acts.wait()
    gathers = []
    for p in range(pieces):
        cols = pl.ds(p * step, step)
        gathered[me, :, cols] = jnp.dot(
            select_b, acts_v[:, cols], preferred_element_type=jnp.float32
        ).astype(jnp.bfloat16)
        for k in range(1, peers):
            copy = pltpu.make_async_remote_copy(
                src_ref=gathered.at[me, :, cols],
                dst_ref=gathered.at[me, :, cols],
                send_sem=gather_send_sem.at[p, k],
                recv_sem=gather_recv_sem.at[p, me],
                device_id=(stage, lax.rem(me + k, peers)),
                device_id_type=MESH,
            )
            copy.start()
            gathers.append(copy)
    table = pltpu.make_async_remote_copy(
        src_ref=table_send,
        dst_ref=table_recv,
        send_sem=table_sem.at[0],
        recv_sem=table_sem.at[1],
        device_id=(after, me),
        device_id_type=MESH,
    )
    table.start()
    total = None
    for p in range(pieces):
        cols = pl.ds(p * step, step)
        gate_up_loads[p].wait()
        for k in range(1, peers):
            source = lax.rem(me + k, peers)
            pltpu.make_async_remote_copy(
                src_ref=gathered.at[source, :, cols],
                dst_ref=gathered.at[source, :, cols],
                send_sem=gather_send_sem.at[p, k],
                recv_sem=gather_recv_sem.at[p, source],
                device_id=(stage, source),
                device_id_type=MESH,
            ).wait_recv()
        rows = (
            gathered[:, :, cols]
            .astype(jnp.float32)
            .reshape(peers * CAP, step)
            .astype(jnp.bfloat16)
        )
        term = jnp.dot(
            rows, gate_up_v[pl.ds(p * step, step), :], preferred_element_type=jnp.float32
        )
        total = term if total is None else total + term
    gate = total[:, :hid]
    up = total[:, hid:]
    hidden = (gate / (1.0 + jnp.exp(-gate)) * up).astype(jnp.bfloat16)

    load_down.wait()
    for p in range(pieces):
        cols = pl.ds(p * step, step)
        part = jnp.dot(hidden, down_v[:, cols], preferred_element_type=jnp.float32)
        part_send[:, :, cols] = part.reshape(peers, CAP, step).astype(jnp.bfloat16)
        for k in range(1, peers):
            owner = lax.rem(me + k, peers)
            pltpu.make_async_remote_copy(
                src_ref=part_send.at[owner, :, cols],
                dst_ref=part_recv.at[me, :, cols],
                send_sem=part_send_sem.at[p, k],
                recv_sem=part_recv_sem.at[p, me],
                device_id=(stage, owner),
                device_id_type=MESH,
            ).start()

    forwards = []
    for p in range(pieces):
        cols = pl.ds(p * step, step)
        merged = part_send[me, :, cols].astype(jnp.float32)
        for k in range(1, peers):
            source = lax.rem(me + k, peers)
            pltpu.make_async_remote_copy(
                src_ref=part_send.at[source, :, cols],
                dst_ref=part_recv.at[source, :, cols],
                send_sem=part_send_sem.at[p, k],
                recv_sem=part_recv_sem.at[p, source],
                device_id=(stage, source),
                device_id_type=MESH,
            ).wait_recv()
            merged = merged + part_recv[source, :, cols].astype(jnp.float32)
        rows_send[:, cols] = (merged * slot_coeff).astype(jnp.bfloat16)
        forward = pltpu.make_async_remote_copy(
            src_ref=rows_send.at[:, cols],
            dst_ref=rows_recv.at[:, cols],
            send_sem=rows_sem.at[0, p],
            recv_sem=rows_sem.at[1, p],
            device_id=(after, me),
            device_id_type=MESH,
        )
        forward.start()
        forwards.append(forward)

    for copy in gathers:
        copy.wait_send()
    for p in range(pieces):
        for k in range(1, peers):
            owner = lax.rem(me + k, peers)
            pltpu.make_async_remote_copy(
                src_ref=part_send.at[owner, :, pl.ds(p * step, step)],
                dst_ref=part_recv.at[me, :, pl.ds(p * step, step)],
                send_sem=part_send_sem.at[p, k],
                recv_sem=part_recv_sem.at[p, me],
                device_id=(stage, owner),
                device_id_type=MESH,
            ).wait_send()
    table.wait()
    for forward in forwards:
        forward.wait()
    for p in range(row_pieces):
        span = pl.ds(p * row_step, row_step)
        streams[p].wait()
        layer = lax.dot_general(
            table_recv[:, span],
            rows_recv[...],
            (((0,), (0,)), ((), ())),
            preferred_element_type=jnp.float32,
        )
        out[0, span, :] = (landed[0, span, :].astype(jnp.float32) + layer).astype(out.dtype)


def per_device(stages, peers, acts, routing, combine_w, w_gate_up, w_down):
    _, tokens, width = acts.shape
    routing = jnp.swapaxes(routing, 1, 2)
    combine_w = jnp.swapaxes(combine_w, 1, 2)
    pieces = pieces_of(width)
    row_pieces = 1
    anywhere = pl.BlockSpec(memory_space=pl.ANY)
    in_vmem = pl.BlockSpec(memory_space=pltpu.VMEM)
    dma = pltpu.SemaphoreType.DMA
    return pl.pallas_call(
        functools.partial(kernel, stages, peers, pieces, row_pieces),
        out_shape=pltpu.VMEM(acts.shape, acts.dtype),
        in_specs=[anywhere] * 5,
        out_specs=in_vmem,
        scratch_shapes=[
            pltpu.VMEM(acts.shape, acts.dtype),
            pltpu.VMEM((tokens, width), acts.dtype),
            pltpu.VMEM(routing.shape[1:], routing.dtype),
            pltpu.VMEM(combine_w.shape[1:], combine_w.dtype),
            pltpu.VMEM(w_gate_up.shape[1:], w_gate_up.dtype),
            pltpu.VMEM(w_down.shape[1:], w_down.dtype),
            pltpu.VMEM((peers, CAP, width), jnp.bfloat16),
            pltpu.VMEM((peers, CAP, width), jnp.bfloat16),
            pltpu.VMEM((peers, CAP, width), jnp.bfloat16),
            pltpu.VMEM((CAP, width), jnp.bfloat16),
            pltpu.VMEM((CAP, width), jnp.bfloat16),
            pltpu.VMEM((CAP, tokens), jnp.bfloat16),
            pltpu.VMEM((CAP, tokens), jnp.bfloat16),
            dma((3,)),
            dma((pieces,)),
            dma,
            dma((2, row_pieces)),
            dma((2,)),
            dma((pieces, peers)),
            dma((pieces, peers)),
            dma((pieces, peers)),
            dma((pieces, peers)),
            dma((2, pieces)),
        ],
        compiler_params=pltpu.CompilerParams(collective_id=0, has_side_effects=True),
        name="relay_tick",
    )(acts, routing, combine_w, w_gate_up, w_down)


def solution(mesh):
    return jax.shard_map(
        functools.partial(per_device, mesh.shape["pipe"], mesh.shape["expert"]),
        mesh=mesh,
        in_specs=(
            P("pipe", "expert", None),
            P("pipe", "expert", None),
            P("pipe", "expert", None),
            P("pipe", None, "expert"),
            P("pipe", "expert", None),
        ),
        out_specs=P("pipe", "expert", None),
        check_vma=False,
    )
```

```python
import functools

import jax
import jax.numpy as jnp
from jax import lax
from jax.experimental import pallas as pl
from jax.experimental.pallas import tpu as pltpu
from jax.sharding import PartitionSpec as P

CAP = 8
MESH = pl.DeviceIdType.MESH


def kernel(
    stages,
    peers,
    pieces,
    row_pieces,
    acts,
    routing,
    combine_w,
    w_gate_up,
    w_down,
    out,
    landed,
    acts_v,
    route_v,
    mix_v,
    gate_up_v,
    down_v,
    gathered,
    part_send,
    part_recv,
    rows_send,
    rows_recv,
    load_sem,
    gate_up_sem,
    down_sem,
    stream_sem,
    gather_send_sem,
    gather_recv_sem,
    part_send_sem,
    part_recv_sem,
    rows_sem,
):
    stage = lax.axis_index("pipe")
    me = lax.axis_index("expert")
    after = lax.rem(stage + 1, stages)
    before = lax.rem(stage + stages - 1, stages)
    width = acts.shape[2]
    tokens = acts.shape[1]
    hid = w_down.shape[1]
    step = width // pieces
    row_step = tokens // row_pieces

    barrier = pltpu.get_barrier_semaphore()
    for k in range(1, peers):
        pl.semaphore_signal(
            barrier, inc=1, device_id=(stage, lax.rem(me + k, peers)), device_id_type=MESH
        )
    pl.semaphore_signal(barrier, inc=1, device_id=(before, me), device_id_type=MESH)
    pl.semaphore_signal(barrier, inc=1, device_id=(after, me), device_id_type=MESH)

    load_route = pltpu.make_async_copy(routing.at[0], route_v, load_sem.at[0])
    load_mix = pltpu.make_async_copy(combine_w.at[0], mix_v, load_sem.at[1])
    load_acts = pltpu.make_async_copy(acts.at[0], acts_v, load_sem.at[2])
    load_route.start()
    load_mix.start()
    load_acts.start()
    gate_up_loads = []
    for p in range(pieces):
        rows = pl.ds(p * step, step)
        load = pltpu.make_async_copy(
            w_gate_up.at[0, rows, :], gate_up_v.at[rows, :], gate_up_sem.at[p]
        )
        load.start()
        gate_up_loads.append(load)
    load_down = pltpu.make_async_copy(w_down.at[0], down_v, down_sem)
    load_down.start()

    pl.semaphore_wait(barrier, peers + 1)
    streams = []
    for p in range(row_pieces):
        span = pl.ds(p * row_step, row_step)
        stream = pltpu.make_async_remote_copy(
            src_ref=acts.at[:, span, :],
            dst_ref=landed.at[:, span, :],
            send_sem=stream_sem.at[0, p],
            recv_sem=stream_sem.at[1, p],
            device_id=(after, me),
            device_id_type=MESH,
        )
        stream.start()
        streams.append(stream)

    load_route.wait()
    load_mix.wait()
    named = route_v[...] == 0
    chosen = jnp.max(jnp.where(named, 1.0, 0.0), axis=0, keepdims=True)
    coefficient = jnp.sum(jnp.where(named, mix_v[...], 0.0), axis=0, keepdims=True)
    earlier = (
        lax.broadcasted_iota(jnp.int32, (tokens, tokens), 0)
        <= lax.broadcasted_iota(jnp.int32, (tokens, tokens), 1)
    ).astype(jnp.float32)
    count = jnp.dot(
        jnp.broadcast_to(chosen, (CAP, tokens)), earlier, preferred_element_type=jnp.float32
    )
    slot = lax.broadcasted_iota(jnp.int32, (CAP, tokens), 0).astype(jnp.float32) + 1.0
    select = jnp.where((count == slot) & (chosen > 0.5), 1.0, 0.0)
    slot_coeff = jnp.sum(select * coefficient, axis=1, keepdims=True)
    select_b = select.astype(jnp.bfloat16)
    rows_send[:, pl.ds(width, tokens)] = select_b

    load_acts.wait()
    gathers = []
    for p in range(pieces):
        cols = pl.ds(p * step, step)
        gathered[me, :, cols] = jnp.dot(
            select_b, acts_v[:, cols], preferred_element_type=jnp.float32
        ).astype(jnp.bfloat16)
        for k in range(1, peers):
            copy = pltpu.make_async_remote_copy(
                src_ref=gathered.at[me, :, cols],
                dst_ref=gathered.at[me, :, cols],
                send_sem=gather_send_sem.at[p, k],
                recv_sem=gather_recv_sem.at[p, me],
                device_id=(stage, lax.rem(me + k, peers)),
                device_id_type=MESH,
            )
            copy.start()
            gathers.append(copy)
    total = None
    for p in range(pieces):
        cols = pl.ds(p * step, step)
        gate_up_loads[p].wait()
        for k in range(1, peers):
            source = lax.rem(me + k, peers)
            pltpu.make_async_remote_copy(
                src_ref=gathered.at[source, :, cols],
                dst_ref=gathered.at[source, :, cols],
                send_sem=gather_send_sem.at[p, k],
                recv_sem=gather_recv_sem.at[p, source],
                device_id=(stage, source),
                device_id_type=MESH,
            ).wait_recv()
        rows = (
            gathered[:, :, cols]
            .astype(jnp.float32)
            .reshape(peers * CAP, step)
            .astype(jnp.bfloat16)
        )
        term = jnp.dot(
            rows, gate_up_v[pl.ds(p * step, step), :], preferred_element_type=jnp.float32
        )
        total = term if total is None else total + term
    gate = total[:, :hid]
    up = total[:, hid:]
    hidden = (gate / (1.0 + jnp.exp(-gate)) * up).astype(jnp.bfloat16)

    load_down.wait()
    for p in range(pieces):
        cols = pl.ds(p * step, step)
        part = jnp.dot(hidden, down_v[:, cols], preferred_element_type=jnp.float32)
        part_send[:, :, cols] = part.reshape(peers, CAP, step).astype(jnp.bfloat16)
        for k in range(1, peers):
            owner = lax.rem(me + k, peers)
            pltpu.make_async_remote_copy(
                src_ref=part_send.at[owner, :, cols],
                dst_ref=part_recv.at[me, :, cols],
                send_sem=part_send_sem.at[p, k],
                recv_sem=part_recv_sem.at[p, me],
                device_id=(stage, owner),
                device_id_type=MESH,
            ).start()

    for p in range(pieces):
        cols = pl.ds(p * step, step)
        merged = part_send[me, :, cols].astype(jnp.float32)
        for k in range(1, peers):
            source = lax.rem(me + k, peers)
            pltpu.make_async_remote_copy(
                src_ref=part_send.at[source, :, cols],
                dst_ref=part_recv.at[source, :, cols],
                send_sem=part_send_sem.at[p, k],
                recv_sem=part_recv_sem.at[p, source],
                device_id=(stage, source),
                device_id_type=MESH,
            ).wait_recv()
            merged = merged + part_recv[source, :, cols].astype(jnp.float32)
        rows_send[:, cols] = (merged * slot_coeff).astype(jnp.bfloat16)
    forward = pltpu.make_async_remote_copy(
        src_ref=rows_send,
        dst_ref=rows_recv,
        send_sem=rows_sem.at[0],
        recv_sem=rows_sem.at[1],
        device_id=(after, me),
        device_id_type=MESH,
    )
    forward.start()

    for copy in gathers:
        copy.wait_send()
    for p in range(pieces):
        for k in range(1, peers):
            owner = lax.rem(me + k, peers)
            pltpu.make_async_remote_copy(
                src_ref=part_send.at[owner, :, pl.ds(p * step, step)],
                dst_ref=part_recv.at[me, :, pl.ds(p * step, step)],
                send_sem=part_send_sem.at[p, k],
                recv_sem=part_recv_sem.at[p, me],
                device_id=(stage, owner),
                device_id_type=MESH,
            ).wait_send()
    forward.wait()
    for p in range(row_pieces):
        span = pl.ds(p * row_step, row_step)
        streams[p].wait()
        layer = lax.dot_general(
            rows_recv[:, pl.ds(width + p * row_step, row_step)],
            rows_recv[:, pl.ds(0, width)],
            (((0,), (0,)), ((), ())),
            preferred_element_type=jnp.float32,
        )
        out[0, span, :] = (landed[0, span, :].astype(jnp.float32) + layer).astype(out.dtype)


def per_device(stages, peers, acts, routing, combine_w, w_gate_up, w_down):
    _, tokens, width = acts.shape
    routing = jnp.swapaxes(routing, 1, 2)
    combine_w = jnp.swapaxes(combine_w, 1, 2)
    pieces = 1
    row_pieces = 1
    anywhere = pl.BlockSpec(memory_space=pl.ANY)
    in_vmem = pl.BlockSpec(memory_space=pltpu.VMEM)
    dma = pltpu.SemaphoreType.DMA
    return pl.pallas_call(
        functools.partial(kernel, stages, peers, pieces, row_pieces),
        out_shape=pltpu.VMEM(acts.shape, acts.dtype),
        in_specs=[anywhere] * 5,
        out_specs=in_vmem,
        scratch_shapes=[
            pltpu.VMEM(acts.shape, acts.dtype),
            pltpu.VMEM((tokens, width), acts.dtype),
            pltpu.VMEM(routing.shape[1:], routing.dtype),
            pltpu.VMEM(combine_w.shape[1:], combine_w.dtype),
            pltpu.VMEM(w_gate_up.shape[1:], w_gate_up.dtype),
            pltpu.VMEM(w_down.shape[1:], w_down.dtype),
            pltpu.VMEM((peers, CAP, width), jnp.bfloat16),
            pltpu.VMEM((peers, CAP, width), jnp.bfloat16),
            pltpu.VMEM((peers, CAP, width), jnp.bfloat16),
            pltpu.VMEM((CAP, width + tokens), jnp.bfloat16),
            pltpu.VMEM((CAP, width + tokens), jnp.bfloat16),
            dma((3,)),
            dma((pieces,)),
            dma,
            dma((2, row_pieces)),
            dma((pieces, peers)),
            dma((pieces, peers)),
            dma((pieces, peers)),
            dma((pieces, peers)),
            dma((2,)),
        ],
        compiler_params=pltpu.CompilerParams(collective_id=0, has_side_effects=True),
        name="relay_tick",
    )(acts, routing, combine_w, w_gate_up, w_down)


def solution(mesh):
    return jax.shard_map(
        functools.partial(per_device, mesh.shape["pipe"], mesh.shape["expert"]),
        mesh=mesh,
        in_specs=(
            P("pipe", "expert", None),
            P("pipe", "expert", None),
            P("pipe", "expert", None),
            P("pipe", None, "expert"),
            P("pipe", "expert", None),
        ),
        out_specs=P("pipe", "expert", None),
        check_vma=False,
    )
```
